256 devices in a mesh: src: 8 (over y, core), snk: 32 (over x, z).
Axes of the slice: x: 4, y: 4, z: 8, core: 2. Of those that a mesh axis runs over, the one named last changes fastest.
Arguments:
- peram: bfloat16 [8, 32, 2, 256, 256], P('src', None, None, None, 'snk'), may hold values from -6 to 6
- meson_blocks: bfloat16 [32, 4, 2, 256, 256], P('snk'), may hold values from -0.25 to 0.25
- edge_left: int32 [8, 32, 32], P('src', 'snk'), may hold values from 0 to 3
- edge_right: int32 [8, 32, 32], P('src', 'snk'), may hold values from 0 to 3
- edge_node: int32 [8, 32, 32], P('src', 'snk'), may hold values from 0 to 4
- edge_weight: int32 [8, 32, 32], P('src', 'snk'), may hold values from 0 to 15
- weight_table: float32 [16, 2], replicated, may hold values from -0.2 to 0.2
Outputs:
- node_matrices: bfloat16 [256, 4, 2, 256], P('snk')
The draws below stay inside these ranges and needn't reach their ends.
Inputs may be any that keep to these rules, and one draw needn't show every extreme that they name: `edge_node`: the value 4 marks an empty slot that feeds no node.
All inputs are finite; a program needn't handle non-finite values.
Results may differ from the reference program's by a relative error of at most 0.009.
Values may be sent and summed in bfloat16 or wider, within the bound.
No kernel may reach another device: no remote copies, remote signals or barrier semaphores. Data moves between devices by JAX's collectives and lax.ppermute only.
A program may use at most 128 MiB of HBM per device.

```python
import jax
import jax.numpy as jnp
from jax import lax

N = 256
MOM = 4
E_DEV = 32
NODES = 4
NW = 16
NS = 8
NT = 32
N_SRC = 8
N_SNK = 32


def with_ends(drawn, stream_key, least, largest):
    place = [jax.random.randint(jax.random.fold_in(stream_key, axis), (), 0, length) for axis, length in enumerate(drawn.shape)]
    widest = drawn.shape.index(max(drawn.shape))
    beside = place[:widest] + [(place[widest] + 1) % drawn.shape[widest]] + place[widest + 1:]
    return drawn.at[tuple(place)].set(least).at[tuple(beside)].set(largest)


def block_levels(own_key, extent, pieces, smallest, top_value):
    def one(position, blocks):
        draws = jax.random.uniform(jax.random.fold_in(jax.random.fold_in(own_key, 6), position), (blocks,), jnp.float32, smallest / len(pieces), top_value / len(pieces))
        return jnp.repeat(jnp.exp(draws), extent[position] // blocks).reshape((-1,) + (1,) * (len(extent) - position - 1))

    gain = one(*pieces[0])
    for cut in pieces[1:]:
        gain = gain * one(*cut)
    return gain


def scatter_about(own_key, extent, width, reach, pieces=(), kind=jnp.bfloat16):
    entries = width * jax.random.normal(own_key, extent, jnp.float32)
    if pieces:
        entries = entries * block_levels(own_key, extent, pieces, -0.22, 0.18)
    return jnp.clip(entries, -reach, reach).astype(kind)


def setup_inputs(seed: int = 0) -> dict:
    seeds = jax.random.split(jax.random.key(seed), 8)
    peram = scatter_about(seeds[0], (NS, NT, 2, N, N), 1.0, 6.0, ((0, 8), (4, 32)))
    meson_blocks = scatter_about(seeds[1], (NT, MOM, 2, N, N), (2 * N) ** -0.5, 0.25, ((0, 32),))
    edge_left = with_ends(jax.random.randint(seeds[2], (NS, NT, E_DEV), 0, MOM), jax.random.fold_in(seeds[2], 1), 0, MOM - 1).astype(jnp.int32)
    edge_right = with_ends(jax.random.randint(seeds[3], (NS, NT, E_DEV), 0, MOM), jax.random.fold_in(seeds[3], 1), 0, MOM - 1).astype(jnp.int32)
    edge_node = with_ends(jax.random.randint(seeds[4], (NS, NT, E_DEV), 0, NODES + 1), jax.random.fold_in(seeds[4], 1), 0, NODES).astype(jnp.int32)
    edge_weight = with_ends(jax.random.randint(seeds[5], (NS, NT, E_DEV), 0, NW), jax.random.fold_in(seeds[5], 1), 0, NW - 1).astype(jnp.int32)
    weight_table = scatter_about(seeds[6], (NW, 2), 0.03, 0.2, (), jnp.float32)
    return dict(peram=peram, meson_blocks=meson_blocks, edge_left=edge_left, edge_right=edge_right, edge_node=edge_node, edge_weight=edge_weight, weight_table=weight_table)


def block_products(blocks, whole_peram):
    number = blocks.shape[0]
    order = blocks.shape[2]
    left_real = blocks[:, 0].reshape(number * order, order)
    left_imag = blocks[:, 1].reshape(number * order, order)
    real_part = jnp.dot(left_real, whole_peram[0], preferred_element_type=jnp.float32) - jnp.dot(left_imag, whole_peram[1], preferred_element_type=jnp.float32)
    imag_part = jnp.dot(left_real, whole_peram[1], preferred_element_type=jnp.float32) + jnp.dot(left_imag, whole_peram[0], preferred_element_type=jnp.float32)
    stacked = jnp.stack([real_part.reshape(number, order, order), imag_part.reshape(number, order, order)], 1)
    return stacked.astype(jnp.bfloat16)


def reference(peram, meson_blocks, edge_left, edge_right, edge_node, edge_weight, weight_table):
    high = lax.Precision.HIGHEST
    time_stride = N_SNK // N_SRC
    node_ids = jnp.arange(NODES, dtype=jnp.int32)
    block_ids = jnp.arange(MOM, dtype=jnp.int32)
    table_ids = jnp.arange(NW, dtype=jnp.int32)

    def one_time(running, inputs):
        whole_peram, blocks, left_of, right_of, node_of, weight_of = inputs
        left_times = block_products(blocks, whole_peram).astype(jnp.float32)
        pick_weight = (weight_of[:, None] == table_ids[None, :]).astype(jnp.float32)
        edge_coef = jnp.dot(pick_weight, weight_table, precision=high)
        member = (node_of[:, None] == node_ids[None, :]).astype(jnp.float32)
        pick_right = (right_of[:, None] == block_ids[None, :]).astype(jnp.float32)
        pick_left = (left_of[:, None] == block_ids[None, :]).astype(jnp.float32)
        mix_real = jnp.einsum("en,eb,ea->nba", member * edge_coef[:, 0:1], pick_right, pick_left, precision=high)
        mix_imag = jnp.einsum("en,eb,ea->nba", member * edge_coef[:, 1:2], pick_right, pick_left, precision=high)
        pair_real = jnp.einsum("nba,aij->nbij", mix_real, left_times[:, 0], precision=high) - jnp.einsum("nba,aij->nbij", mix_imag, left_times[:, 1], precision=high)
        pair_imag = jnp.einsum("nba,aij->nbij", mix_real, left_times[:, 1], precision=high) + jnp.einsum("nba,aij->nbij", mix_imag, left_times[:, 0], precision=high)
        return (running[0] + pair_real, running[1] + pair_imag), None

    def one_source(inputs):
        source_index, peram_s, left_s, right_s, node_s, weight_s = inputs
        empty_sums = jnp.zeros((NODES, MOM, N, N), jnp.float32)
        sums, unused = lax.scan(one_time, (empty_sums, empty_sums), (peram_s, meson_blocks, left_s, right_s, node_s, weight_s))
        right_f = lax.dynamic_index_in_dim(meson_blocks, (source_index * time_stride).astype(jnp.int32), 0, keepdims=False).astype(jnp.float32)
        out_real = jnp.einsum("nbij,bjk->nik", sums[0], right_f[:, 0], precision=high) - jnp.einsum("nbij,bjk->nik", sums[1], right_f[:, 1], precision=high)
        out_imag = jnp.einsum("nbij,bjk->nik", sums[0], right_f[:, 1], precision=high) + jnp.einsum("nbij,bjk->nik", sums[1], right_f[:, 0], precision=high)
        return jnp.stack([out_real, out_imag], 1)

    per_source = lax.map(one_source, (jnp.arange(N_SRC, dtype=jnp.int32), peram, edge_left, edge_right, edge_node, edge_weight))
    summed = jnp.sum(per_source, axis=0)
    return jnp.transpose(summed, (2, 0, 1, 3)).astype(jnp.bfloat16)
```

```python
import functools

import jax
import jax.numpy as jnp
from jax import lax
from jax.experimental import pallas as pl
from jax.experimental.pallas import tpu as pltpu
from jax.sharding import Mesh, PartitionSpec as P


N = 256
MOM = 4
EDGES = 32
NODES = 4
SNK = 32
ROWS = N // SNK
DEEP = MOM * 2 * N
ALL = ("y", "core", "x", "z")
NY, NC, NX, NZ = 4, 2, 4, 8
BF16 = jnp.bfloat16
F32 = jnp.float32
VMEM_CAP = 14 * 2**20


def mix_kernel(keep, left_e, right_e, node_e, weight_e, table, blocks, mixed, gain):
    core = lax.axis_index("core")
    first = 2 * (core if keep else 1 - core)
    shift = lax.axis_index("x") - lax.axis_index("y") + 2 * NX

    def clear(i, carry):
        gain[0, i] = 0.0
        gain[1, i] = 0.0
        return carry

    lax.fori_loop(0, (NODES + 1) * 16, clear, 0)

    def gather(e, carry):
        key = node_e[0, 0, e] * 16 + right_e[0, 0, e] * 4 + left_e[0, 0, e]
        w = weight_e[0, 0, e]
        gain[0, key] = gain[0, key] + table[0, w]
        gain[1, key] = gain[1, key] + table[1, w]
        return carry

    lax.fori_loop(0, EDGES, gather, 0)
    step = 16

    def rows(r, carry):
        here = pl.ds(pl.multiple_of(r * step, step), step)
        real = [blocks[0, a, 0, here, :].astype(F32) for a in range(MOM)]
        imag = [blocks[0, a, 1, here, :].astype(F32) for a in range(MOM)]
        for n in range(2):
            for d in range(MOM):
                base = (first + n) * 16 + lax.rem(shift - d, MOM) * 4
                wr = [gain[0, base + a] for a in range(MOM)]
                wi = [gain[1, base + a] for a in range(MOM)]
                sum_r = wr[0] * real[0] - wi[0] * imag[0]
                sum_i = wr[0] * imag[0] + wi[0] * real[0]
                for a in range(1, MOM):
                    sum_r = sum_r + (wr[a] * real[a] - wi[a] * imag[a])
                    sum_i = sum_i + (wr[a] * imag[a] + wi[a] * real[a])
                mixed[n, here, (2 * d) * N : (2 * d + 1) * N] = sum_r.astype(BF16)
                mixed[n, here, (2 * d + 1) * N : (2 * d + 2) * N] = sum_i.astype(BF16)
        return carry

    lax.fori_loop(0, N // step, rows, 0)


def mix(keep, left, right, node, weight, table, blocks):
    smem = pl.BlockSpec(memory_space=pltpu.SMEM)
    vmem = pl.BlockSpec(memory_space=pltpu.VMEM)
    return pl.pallas_call(
        functools.partial(mix_kernel, keep),
        out_shape=jax.ShapeDtypeStruct((2, N, DEEP), BF16),
        in_specs=[smem] * 5 + [vmem],
        out_specs=vmem,
        scratch_shapes=[pltpu.SMEM((2, 128), F32)],
        cost_estimate=pl.CostEstimate(
            flops=2 * MOM * MOM * 8 * N * N,
            bytes_accessed=(MOM * 2 + 2 * MOM * 2) * N * N * 2,
            transcendentals=0,
        ),
        name="mix_keep" if keep else "mix_send",
    )(left, right, node, weight, table, blocks)


def half_product(mixed, stack, out):
    parts = [
        jnp.dot(mixed[n], stack[...], preferred_element_type=F32).reshape(SNK, ROWS, 2 * N)
        for n in range(2)
    ]
    out[...] = jnp.concatenate(parts, 1).astype(out.dtype)


def send_kernel(tau_t, r0, r1, r2, r3, mixed, send, stack):
    tau = [
        tau_t[:, p].astype(F32).reshape(N, N).T.astype(BF16) for p in range(2)
    ]
    for d, block in enumerate((r0, r1, r2, r3)):
        real = jnp.dot(tau[0], block[0], preferred_element_type=F32) - jnp.dot(
            tau[1], block[1], preferred_element_type=F32
        )
        imag = jnp.dot(tau[0], block[1], preferred_element_type=F32) + jnp.dot(
            tau[1], block[0], preferred_element_type=F32
        )
        top, low = 2 * d * N, (2 * d + 1) * N
        stack[top : top + N, :N] = real.astype(BF16)
        stack[top : top + N, N:] = imag.astype(BF16)
        stack[low : low + N, :N] = (-imag).astype(BF16)
        stack[low : low + N, N:] = real.astype(BF16)
    half_product(mixed, stack, send)


def send_half(tau_t, right, mixed):
    vmem = pl.BlockSpec(memory_space=pltpu.VMEM)
    return pl.pallas_call(
        send_kernel,
        out_shape=(
            jax.ShapeDtypeStruct((SNK, 2 * ROWS, 2 * N), BF16),
            jax.ShapeDtypeStruct((DEEP, 2 * N), BF16),
        ),
        in_specs=[vmem] * 6,
        out_specs=(vmem, vmem),
        compiler_params=pltpu.CompilerParams(vmem_limit_bytes=VMEM_CAP),
        cost_estimate=pl.CostEstimate(
            flops=2 * (MOM * 4 + 2 * MOM * 4) * N * N * N,
            bytes_accessed=6 * 2**20,
            transcendentals=0,
        ),
        name="send_half",
    )(tau_t, *right, mixed)


def keep_half(mixed, stack):
    vmem = pl.BlockSpec(memory_space=pltpu.VMEM)
    return pl.pallas_call(
        half_product,
        out_shape=jax.ShapeDtypeStruct((SNK, 2 * ROWS, 2 * N), F32),
        in_specs=[vmem] * 2,
        out_specs=vmem,
        compiler_params=pltpu.CompilerParams(vmem_limit_bytes=VMEM_CAP),
        cost_estimate=pl.CostEstimate(
            flops=2 * 2 * MOM * 4 * N * N * N,
            bytes_accessed=5 * 2**20,
            transcendentals=0,
        ),
        name="keep_half",
    )(mixed, stack)


def device(y, c, x, z):
    return ((y * NC + c) * NX + x % NX) * NZ + z % NZ


def spread(block):
    x, z = lax.axis_index("x"), lax.axis_index("z")
    y, c = lax.axis_index("y"), lax.axis_index("core")
    lines = [(a, b, i) for a in range(NY) for b in range(NC) for i in range(NX)]

    def along_z(value, hops):
        pairs = [
            (device(a, b, i, 4 * b + u), device(a, b, i, 4 * b + v))
            for a, b, i in lines
            for u, v in hops
        ]
        return lax.ppermute(value, ALL, pairs)

    def home(value, k):
        pairs = [
            (device(b, c, a, j), device(a, c, b + k, j))
            for a in range(NX)
            for b in range(NY)
            for c in range(NC)
            for j in range(NZ)
        ]
        return lax.ppermute(value, ALL, pairs)

    where_z = lax.rem(z - 4 * c + NZ, NZ)
    own = lax.dynamic_index_in_dim(block, lax.rem(y - x + NX, NX), 0, keepdims=False)
    got = []
    for d in (4, 3, 5, 2, 6, 1, 7):
        got.append(along_z(own, [(0, d)]))
    part = jnp.where(where_z == 0, own, functools.reduce(jnp.add, got))
    pieces = []
    for k in range(NX):
        pieces.append(home(part, k))
    return pieces


def shards(peram, meson_blocks, edge_left, edge_right, edge_node, edge_weight, weight_table):
    return contract(
        peram,
        meson_blocks,
        (edge_left, edge_right, edge_node, edge_weight, weight_table.T),
    )


def contract(peram, meson_blocks, edges):
    core = lax.axis_index("core")
    by_time = jnp.swapaxes(peram[0], 2, 3)
    tau_t = lax.all_to_all(by_time, ("x", "z"), split_axis=0, concat_axis=0, tiled=True)
    mixed_send = mix(False, *edges, meson_blocks)
    mixed_keep = mix(True, *edges, meson_blocks)
    right = spread(meson_blocks[0])
    send, stack = send_half(tau_t, right, mixed_send)
    got = lax.ppermute(send, "core", [(0, 1), (1, 0)])
    keep = keep_half(mixed_keep, stack)
    pair = (keep + got.astype(F32)).astype(BF16)
    times = lax.all_to_all(pair, ("x", "z"), split_axis=0, concat_axis=0, tiled=True)
    one = jnp.sum(times.astype(F32), 0)
    total = one
    for d in range(1, NY):
        total = total + lax.ppermute(one, "y", [(i, (i + d) % NY) for i in range(NY)])
    mine = total.astype(BF16)
    other = lax.ppermute(mine, "core", [(0, 1), (1, 0)])
    halves = jnp.where(core == 0, jnp.stack([mine, other]), jnp.stack([other, mine]))
    halves = halves.reshape(2, 2, ROWS, 2, N)
    return jnp.transpose(halves, (2, 0, 1, 3, 4)).reshape(ROWS, NODES, 2, N)


def solution(mesh):
    fine = Mesh(mesh.devices.reshape(NY, NC, NX, NZ), ALL)
    src, snk = ("y", "core"), ("x", "z")
    edges = P(src, snk, None)
    return jax.shard_map(
        shards,
        mesh=fine,
        in_specs=(
            P(src, None, None, None, snk),
            P(snk, None, None, None, None),
            edges,
            edges,
            edges,
            edges,
            P(),
        ),
        out_specs=P(snk, None, None, None),
        check_vma=False,
    )
```

```python
import functools

import jax
import jax.numpy as jnp
from jax import lax
from jax.experimental import pallas as pl
from jax.experimental.pallas import tpu as pltpu
from jax.sharding import Mesh, PartitionSpec as P


N = 256
MOM = 4
EDGES = 32
NODES = 4
SNK = 32
ROWS = N // SNK
DEEP = MOM * 2 * N
ALL = ("y", "core", "x", "z")
NY, NC, NX, NZ = 4, 2, 4, 8
BF16 = jnp.bfloat16
F32 = jnp.float32
VMEM_CAP = 48 * 2**20
CHUNK = 64
POSTS = (0, 3)
LINES = ((6, 5), (7, 2), (1, 4))
MIX_CAP = 60 * 2**20
ROUND = (2, 1, 3)


def mix_kernel(left_e, right_e, node_e, weight_e, table, blocks, out, gain):
    core = lax.axis_index("core")
    shift = lax.axis_index("x") - lax.axis_index("y") + 2 * NX

    @pl.when(pl.program_id(0) == 0)
    def fold_edges():
        def clear(i, carry):
            gain[0, i] = 0.0
            gain[1, i] = 0.0
            return carry

        lax.fori_loop(0, (NODES + 1) * 16, clear, 0)

        def gather(e, carry):
            key = node_e[0, 0, e] * 16 + right_e[0, 0, e] * 4 + left_e[0, 0, e]
            w = weight_e[0, 0, e]
            gain[0, key] = gain[0, key] + table[0, w]
            gain[1, key] = gain[1, key] + table[1, w]
            return carry

        lax.fori_loop(0, EDGES, gather, 0)

    step = 16

    def rows(r, carry):
        here = pl.ds(pl.multiple_of(r * step, step), step)
        real = [blocks[0, a, 0, here, :].astype(F32) for a in range(MOM)]
        imag = [blocks[0, a, 1, here, :].astype(F32) for a in range(MOM)]
        both = [u + v for u, v in zip(real, imag)]
        for n in range(NODES):
            for d in range(MOM):
                base = lax.rem(n + 2 - 2 * core, NODES) * 16 + lax.rem(shift - d, MOM) * 4
                wr = [gain[0, base + a] for a in range(MOM)]
                wi = [gain[1, base + a] for a in range(MOM)]
                mid = sum(wr[a] * both[a] for a in range(1, MOM)) + wr[0] * both[0]
                low = sum((wr[a] + wi[a]) * imag[a] for a in range(1, MOM))
                low = low + (wr[0] + wi[0]) * imag[0]
                top = sum((wi[a] - wr[a]) * real[a] for a in range(1, MOM))
                top = top + (wi[0] - wr[0]) * real[0]
                out[n, here, (2 * d) * N : (2 * d + 1) * N] = (mid - low).astype(BF16)
                out[n, here, (2 * d + 1) * N : (2 * d + 2) * N] = (mid + top).astype(BF16)
        return carry

    lax.fori_loop(0, CHUNK // step, rows, 0)


def mix(left, right, node, weight, table, blocks):
    smem = pl.BlockSpec(memory_space=pltpu.SMEM)
    half = pl.BlockSpec((NODES, CHUNK, DEEP), lambda i: (0, i, 0))
    return pl.pallas_call(
        mix_kernel,
        grid=(N // CHUNK,),
        out_shape=jax.ShapeDtypeStruct((NODES, N, DEEP), BF16),
        in_specs=[smem] * 5 + [pl.BlockSpec((1, MOM, 2, CHUNK, N), lambda i: (0, 0, 0, i, 0))],
        out_specs=half,
        scratch_shapes=[pltpu.SMEM((2, 128), F32)],
        compiler_params=pltpu.CompilerParams(vmem_limit_bytes=MIX_CAP),
        cost_estimate=pl.CostEstimate(
            flops=4 * MOM * MOM * 8 * N * N,
            bytes_accessed=(MOM * 2 + 4 * MOM * 2) * N * N * 2,
            transcendentals=0,
        ),
        name="mix",
    )(left, right, node, weight, table, blocks)


def half_product(mixed, stack, out):
    parts = [
        jnp.dot(mixed[n], stack[...], preferred_element_type=F32).reshape(SNK, ROWS, 2 * N)
        for n in range(2)
    ]
    out[...] = jnp.concatenate(parts, 1).astype(out.dtype)


def send_kernel(tau_t, r0, r1, r2, r3, mixed_any, send, stack, mixed, arrived):
    fetch = pltpu.make_async_copy(mixed_any.at[0:2], mixed, arrived)
    fetch.start()
    tau = [
        tau_t[:, p].astype(F32).reshape(N, N).T.astype(BF16) for p in range(2)
    ]
    for d, block in enumerate((r0, r1, r2, r3)):
        real = jnp.dot(tau[0], block[0], preferred_element_type=F32) - jnp.dot(
            tau[1], block[1], preferred_element_type=F32
        )
        imag = jnp.dot(tau[0], block[1], preferred_element_type=F32) + jnp.dot(
            tau[1], block[0], preferred_element_type=F32
        )
        top, low = 2 * d * N, (2 * d + 1) * N
        stack[top : top + N, :N] = real.astype(BF16)
        stack[top : top + N, N:] = imag.astype(BF16)
        stack[low : low + N, :N] = (-imag).astype(BF16)
        stack[low : low + N, N:] = real.astype(BF16)
    fetch.wait()
    half_product(mixed, stack, send)


def send_half(tau_t, right, mixed):
    vmem = pl.BlockSpec(memory_space=pltpu.VMEM)
    return pl.pallas_call(
        send_kernel,
        out_shape=(
            jax.ShapeDtypeStruct((SNK, 2 * ROWS, 2 * N), BF16),
            jax.ShapeDtypeStruct((DEEP, 2 * N), BF16),
        ),
        in_specs=[vmem] * 5 + [pl.BlockSpec(memory_space=pltpu.HBM)],
        out_specs=(vmem, vmem),
        scratch_shapes=[pltpu.VMEM((2, N, DEEP), BF16), pltpu.SemaphoreType.DMA],
        compiler_params=pltpu.CompilerParams(vmem_limit_bytes=VMEM_CAP),
        cost_estimate=pl.CostEstimate(
            flops=2 * (MOM * 4 + 2 * MOM * 4) * N * N * N,
            bytes_accessed=6 * 2**20,
            transcendentals=0,
        ),
        name="send_half",
    )(tau_t, *right, mixed)


def keep_kernel(mixed_far, stack, out, mixed, arrived):
    fetches = [
        pltpu.make_async_copy(mixed_far.at[2 + n], mixed.at[n], arrived.at[n]) for n in range(2)
    ]
    for fetch in fetches:
        fetch.start()
    parts = []
    for n, fetch in enumerate(fetches):
        fetch.wait()
        part = jnp.dot(mixed[n], stack[...], preferred_element_type=F32)
        parts.append(part.reshape(SNK, ROWS, 2 * N))
    out[...] = jnp.concatenate(parts, 1).astype(out.dtype)


def keep_half(mixed, stack):
    vmem = pl.BlockSpec(memory_space=pltpu.VMEM)
    return pl.pallas_call(
        keep_kernel,
        out_shape=jax.ShapeDtypeStruct((SNK, 2 * ROWS, 2 * N), F32),
        in_specs=[pl.BlockSpec(memory_space=pltpu.HBM), vmem],
        out_specs=vmem,
        scratch_shapes=[pltpu.VMEM((2, N, DEEP), BF16), pltpu.SemaphoreType.DMA((2,))],
        compiler_params=pltpu.CompilerParams(vmem_limit_bytes=VMEM_CAP),
        cost_estimate=pl.CostEstimate(
            flops=2 * 2 * MOM * 4 * N * N * N,
            bytes_accessed=5 * 2**20,
            transcendentals=0,
        ),
        name="keep_half",
    )(mixed, stack)


def device(y, c, x, z):
    return ((y * NC + c) * NX + x % NX) * NZ + z % NZ


def spread(block):
    y = lax.axis_index("y")
    lines = [(a, c, b) for a in range(NY) for c in range(NC) for b in range(NX)]
    own = lax.dynamic_index_in_dim(block, y, 0, keepdims=False)
    turns = [
        (device(b, (c + e) % NC, a, 4 * c), device(a, c, a + b, 4 * c + d))
        for a, c, b in lines
        for e, d in enumerate(POSTS)
    ]
    got = [lax.ppermute(own, ALL, turns)]
    for hops in LINES:
        pairs = [
            (device(a, c, b, 4 * c + post), device(a, c, b, 4 * c + d))
            for a, c, b in lines
            for post, d in zip(POSTS, hops)
        ]
        got.append(lax.ppermute(got[0], ALL, pairs))
    part = functools.reduce(jnp.add, got)
    pieces = {0: part}
    for d in ROUND:
        pieces[d] = lax.ppermute(part, "x", [(i, (i + d) % NX) for i in range(NX)])
    return [pieces[d] for d in range(NX)]


def shards(peram, meson_blocks, edge_left, edge_right, edge_node, edge_weight, weight_table):
    return contract(
        peram,
        meson_blocks,
        (edge_left, edge_right, edge_node, edge_weight, weight_table.T),
    )


def contract(peram, meson_blocks, edges):
    core = lax.axis_index("core")
    by_time = jnp.swapaxes(peram[0], 2, 3)
    tau_t = lax.all_to_all(by_time, ("x", "z"), split_axis=0, concat_axis=0, tiled=True)
    mixed = mix(*edges, meson_blocks)
    right = spread(meson_blocks[0])
    send, stack = send_half(tau_t, right, mixed)
    got = lax.ppermute(send, "core", [(0, 1), (1, 0)])
    keep = keep_half(mixed, stack)
    pair = (keep + got.astype(F32)).astype(BF16)
    times = lax.all_to_all(pair, ("x", "z"), split_axis=0, concat_axis=0, tiled=True)
    one = jnp.sum(times.astype(F32), 0)
    total = one
    for d in range(1, NY):
        total = total + lax.ppermute(one, "y", [(i, (i + d) % NY) for i in range(NY)])
    mine = total.astype(BF16)
    other = lax.ppermute(mine, "core", [(0, 1), (1, 0)])
    halves = jnp.where(core == 0, jnp.stack([mine, other]), jnp.stack([other, mine]))
    halves = halves.reshape(2, 2, ROWS, 2, N)
    return jnp.transpose(halves, (2, 0, 1, 3, 4)).reshape(ROWS, NODES, 2, N)


def solution(mesh):
    fine = Mesh(mesh.devices.reshape(NY, NC, NX, NZ), ALL)
    src, snk = ("y", "core"), ("x", "z")
    edges = P(src, snk, None)
    return jax.shard_map(
        shards,
        mesh=fine,
        in_specs=(
            P(src, None, None, None, snk),
            P(snk, None, None, None, None),
            edges,
            edges,
            edges,
            edges,
            P(),
        ),
        out_specs=P(snk, None, None, None),
        check_vma=False,
    )
```

```python
import functools

import jax
import jax.numpy as jnp
from jax import lax
from jax.experimental import pallas as pl
from jax.experimental.pallas import tpu as pltpu
from jax.sharding import Mesh, PartitionSpec as P


N = 256
MOM = 4
EDGES = 32
NODES = 4
SNK = 32
ROWS = N // SNK
DEEP = MOM * 2 * N
ALL = ("y", "core", "x", "z")
NY, NC, NX, NZ = 4, 2, 4, 8
BF16 = jnp.bfloat16
F32 = jnp.float32
VMEM_CAP = 14 * 2**20
CHUNK = 64
POSTS = (0, 3)
LINES = ((1, 4), (7, 2), (6, 5))
MIX_CAP = (8 * 2**20, 60 * 2**20)
ROUND = (1, 3, 2)


def mix_kernel(keep, left_e, right_e, node_e, weight_e, table, blocks, out, gain):
    core = lax.axis_index("core")
    first = 2 * (core if keep else 1 - core)
    shift = lax.axis_index("x") - lax.axis_index("y") + 2 * NX

    @pl.when(pl.program_id(0) == 0)
    def fold_edges():
        def clear(i, carry):
            gain[0, i] = 0.0
            gain[1, i] = 0.0
            return carry

        lax.fori_loop(0, (NODES + 1) * 16, clear, 0)

        def gather(e, carry):
            key = node_e[0, 0, e] * 16 + right_e[0, 0, e] * 4 + left_e[0, 0, e]
            w = weight_e[0, 0, e]
            gain[0, key] = gain[0, key] + table[0, w]
            gain[1, key] = gain[1, key] + table[1, w]
            return carry

        lax.fori_loop(0, EDGES, gather, 0)

    step = 16

    def rows(r, carry):
        here = pl.ds(pl.multiple_of(r * step, step), step)
        real = [blocks[0, a, 0, here, :].astype(F32) for a in range(MOM)]
        imag = [blocks[0, a, 1, here, :].astype(F32) for a in range(MOM)]
        both = [u + v for u, v in zip(real, imag)]
        for n in range(2):
            for d in range(MOM):
                base = (first + n) * 16 + lax.rem(shift - d, MOM) * 4
                wr = [gain[0, base + a] for a in range(MOM)]
                wi = [gain[1, base + a] for a in range(MOM)]
                mid = sum(wr[a] * both[a] for a in range(1, MOM)) + wr[0] * both[0]
                low = sum((wr[a] + wi[a]) * imag[a] for a in range(1, MOM))
                low = low + (wr[0] + wi[0]) * imag[0]
                top = sum((wi[a] - wr[a]) * real[a] for a in range(1, MOM))
                top = top + (wi[0] - wr[0]) * real[0]
                out[n, here, (2 * d) * N : (2 * d + 1) * N] = (mid - low).astype(BF16)
                out[n, here, (2 * d + 1) * N : (2 * d + 2) * N] = (mid + top).astype(BF16)
        return carry

    lax.fori_loop(0, CHUNK // step, rows, 0)


def mix(keep, left, right, node, weight, table, blocks):
    smem = pl.BlockSpec(memory_space=pltpu.SMEM)
    half = pl.BlockSpec((2, CHUNK, DEEP), lambda i: (0, i, 0))
    return pl.pallas_call(
        functools.partial(mix_kernel, keep),
        grid=(N // CHUNK,),
        out_shape=jax.ShapeDtypeStruct((NODES if keep else 2, N, DEEP), BF16),
        in_specs=[smem] * 5 + [pl.BlockSpec((1, MOM, 2, CHUNK, N), lambda i: (0, 0, 0, i, 0))],
        out_specs=half,
        scratch_shapes=[pltpu.SMEM((2, 128), F32)],
        compiler_params=pltpu.CompilerParams(vmem_limit_bytes=MIX_CAP[keep]),
        cost_estimate=pl.CostEstimate(
            flops=2 * MOM * MOM * 8 * N * N,
            bytes_accessed=(MOM * 2 + 2 * MOM * 2) * N * N * 2,
            transcendentals=0,
        ),
        name="mix_keep" if keep else "mix_send",
    )(left, right, node, weight, table, blocks)


def half_product(mixed, stack, out):
    parts = [
        jnp.dot(mixed[n], stack[...], preferred_element_type=F32).reshape(SNK, ROWS, 2 * N)
        for n in range(2)
    ]
    out[...] = jnp.concatenate(parts, 1).astype(out.dtype)


def send_kernel(tau_t, r0, r1, r2, r3, mixed, send, stack):
    tau = [
        tau_t[:, p].astype(F32).reshape(N, N).T.astype(BF16) for p in range(2)
    ]
    for d, block in enumerate((r0, r1, r2, r3)):
        real = jnp.dot(tau[0], block[0], preferred_element_type=F32) - jnp.dot(
            tau[1], block[1], preferred_element_type=F32
        )
        imag = jnp.dot(tau[0], block[1], preferred_element_type=F32) + jnp.dot(
            tau[1], block[0], preferred_element_type=F32
        )
        top, low = 2 * d * N, (2 * d + 1) * N
        stack[top : top + N, :N] = real.astype(BF16)
        stack[top : top + N, N:] = imag.astype(BF16)
        stack[low : low + N, :N] = (-imag).astype(BF16)
        stack[low : low + N, N:] = real.astype(BF16)
    half_product(mixed, stack, send)


def send_half(tau_t, right, mixed):
    vmem = pl.BlockSpec(memory_space=pltpu.VMEM)
    return pl.pallas_call(
        send_kernel,
        out_shape=(
            jax.ShapeDtypeStruct((SNK, 2 * ROWS, 2 * N), BF16),
            jax.ShapeDtypeStruct((DEEP, 2 * N), BF16),
        ),
        in_specs=[vmem] * 6,
        out_specs=(vmem, vmem),
        compiler_params=pltpu.CompilerParams(vmem_limit_bytes=VMEM_CAP),
        cost_estimate=pl.CostEstimate(
            flops=2 * (MOM * 4 + 2 * MOM * 4) * N * N * N,
            bytes_accessed=6 * 2**20,
            transcendentals=0,
        ),
        name="send_half",
    )(tau_t, *right, mixed)


def keep_half(mixed, stack):
    vmem = pl.BlockSpec(memory_space=pltpu.VMEM)
    return pl.pallas_call(
        half_product,
        out_shape=jax.ShapeDtypeStruct((SNK, 2 * ROWS, 2 * N), F32),
        in_specs=[vmem] * 2,
        out_specs=vmem,
        compiler_params=pltpu.CompilerParams(vmem_limit_bytes=VMEM_CAP),
        cost_estimate=pl.CostEstimate(
            flops=2 * 2 * MOM * 4 * N * N * N,
            bytes_accessed=5 * 2**20,
            transcendentals=0,
        ),
        name="keep_half",
    )(mixed, stack)


def device(y, c, x, z):
    return ((y * NC + c) * NX + x % NX) * NZ + z % NZ


def spread(block):
    y = lax.axis_index("y")
    lines = [(a, c, b) for a in range(NY) for c in range(NC) for b in range(NX)]
    own = lax.dynamic_index_in_dim(block, y, 0, keepdims=False)
    turns = [
        (device(b, (c + e) % NC, a, 4 * c), device(a, c, a + b, 4 * c + d))
        for a, c, b in lines
        for e, d in enumerate(POSTS)
    ]
    got = [lax.ppermute(own, ALL, turns)]
    for hops in LINES:
        pairs = [
            (device(a, c, b, 4 * c + post), device(a, c, b, 4 * c + d))
            for a, c, b in lines
            for post, d in zip(POSTS, hops)
        ]
        got.append(lax.ppermute(got[0], ALL, pairs))
    part = functools.reduce(jnp.add, got)
    pieces = {0: part}
    for d in ROUND:
        pieces[d] = lax.ppermute(part, "x", [(i, (i + d) % NX) for i in range(NX)])
    return [pieces[d] for d in range(NX)]


def shards(peram, meson_blocks, edge_left, edge_right, edge_node, edge_weight, weight_table):
    return contract(
        peram,
        meson_blocks,
        (edge_left, edge_right, edge_node, edge_weight, weight_table.T),
    )


def contract(peram, meson_blocks, edges):
    core = lax.axis_index("core")
    by_time = jnp.swapaxes(peram[0], 2, 3)
    tau_t = lax.all_to_all(by_time, ("x", "z"), split_axis=0, concat_axis=0, tiled=True)
    mixed_keep = mix(True, *edges, meson_blocks)
    mixed_send = mix(False, *edges, meson_blocks)
    right = spread(meson_blocks[0])
    send, stack = send_half(tau_t, right, mixed_send)
    got = lax.ppermute(send, "core", [(0, 1), (1, 0)])
    keep = keep_half(mixed_keep, stack)
    pair = (keep + got.astype(F32)).astype(BF16)
    times = lax.all_to_all(pair, ("x", "z"), split_axis=0, concat_axis=0, tiled=True)
    one = jnp.sum(times.astype(F32), 0)
    total = one
    for d in range(1, NY):
        total = total + lax.ppermute(one, "y", [(i, (i + d) % NY) for i in range(NY)])
    mine = total.astype(BF16)
    other = lax.ppermute(mine, "core", [(0, 1), (1, 0)])
    halves = jnp.where(core == 0, jnp.stack([mine, other]), jnp.stack([other, mine]))
    halves = halves.reshape(2, 2, ROWS, 2, N)
    return jnp.transpose(halves, (2, 0, 1, 3, 4)).reshape(ROWS, NODES, 2, N)


def solution(mesh):
    fine = Mesh(mesh.devices.reshape(NY, NC, NX, NZ), ALL)
    src, snk = ("y", "core"), ("x", "z")
    edges = P(src, snk, None)
    return jax.shard_map(
        shards,
        mesh=fine,
        in_specs=(
            P(src, None, None, None, snk),
            P(snk, None, None, None, None),
            edges,
            edges,
            edges,
            edges,
            P(),
        ),
        out_specs=P(snk, None, None, None),
        check_vma=False,
    )
```

```python
import functools

import jax
import jax.numpy as jnp
from jax import lax
from jax.experimental import pallas as pl
from jax.experimental.pallas import tpu as pltpu
from jax.sharding import Mesh, PartitionSpec as P


N = 256
MOM = 4
EDGES = 32
NODES = 4
SNK = 32
ROWS = N // SNK
DEEP = MOM * 2 * N
ALL = ("y", "core", "x", "z")
NY, NC, NX, NZ = 4, 2, 4, 8
BF16 = jnp.bfloat16
F32 = jnp.float32
VMEM_CAP = 14 * 2**20
CHUNK = 64
POSTS = (0, 3)
LINES = ((1, 4), (7, 2), (6, 5))
MIX_CAP = (8 * 2**20, 60 * 2**20)
ROUND = (1, 3, 2)


def mix_kernel(keep, left_e, right_e, node_e, weight_e, table, blocks, out, gain):
    core = lax.axis_index("core")
    first = 2 * (core if keep else 1 - core)
    shift = lax.axis_index("x") - lax.axis_index("y") + 2 * NX

    @pl.when(pl.program_id(0) == 0)
    def fold_edges():
        def clear(i, carry):
            gain[0, i] = 0.0
            gain[1, i] = 0.0
            return carry

        lax.fori_loop(0, (NODES + 1) * 16, clear, 0)

        def gather(e, carry):
            key = node_e[0, 0, e] * 16 + right_e[0, 0, e] * 4 + left_e[0, 0, e]
            w = weight_e[0, 0, e]
            gain[0, key] = gain[0, key] + table[0, w]
            gain[1, key] = gain[1, key] + table[1, w]
            return carry

        lax.fori_loop(0, EDGES, gather, 0)

    step = 16

    def rows(r, carry):
        here = pl.ds(pl.multiple_of(r * step, step), step)
        real = [blocks[0, a, 0, here, :].astype(F32) for a in range(MOM)]
        imag = [blocks[0, a, 1, here, :].astype(F32) for a in range(MOM)]
        both = [u + v for u, v in zip(real, imag)]
        for n in range(2):
            for d in range(MOM):
                base = (first + n) * 16 + lax.rem(shift - d, MOM) * 4
                wr = [gain[0, base + a] for a in range(MOM)]
                wi = [gain[1, base + a] for a in range(MOM)]
                mid = sum(wr[a] * both[a] for a in range(1, MOM)) + wr[0] * both[0]
                low = sum((wr[a] + wi[a]) * imag[a] for a in range(1, MOM))
                low = low + (wr[0] + wi[0]) * imag[0]
                top = sum((wi[a] - wr[a]) * real[a] for a in range(1, MOM))
                top = top + (wi[0] - wr[0]) * real[0]
                out[n, here, (2 * d) * N : (2 * d + 1) * N] = (mid - low).astype(BF16)
                out[n, here, (2 * d + 1) * N : (2 * d + 2) * N] = (mid + top).astype(BF16)
        return carry

    lax.fori_loop(0, CHUNK // step, rows, 0)


def mix(keep, left, right, node, weight, table, blocks):
    smem = pl.BlockSpec(memory_space=pltpu.SMEM)
    half = pl.BlockSpec((2, CHUNK, DEEP), lambda i: (0, i, 0))
    return pl.pallas_call(
        functools.partial(mix_kernel, keep),
        grid=(N // CHUNK,),
        out_shape=jax.ShapeDtypeStruct((NODES if keep else 2, N, DEEP), BF16),
        in_specs=[smem] * 5 + [pl.BlockSpec((1, MOM, 2, CHUNK, N), lambda i: (0, 0, 0, i, 0))],
        out_specs=half,
        scratch_shapes=[pltpu.SMEM((2, 128), F32)],
        compiler_params=pltpu.CompilerParams(vmem_limit_bytes=MIX_CAP[keep]),
        cost_estimate=pl.CostEstimate(
            flops=2 * MOM * MOM * 8 * N * N,
            bytes_accessed=(MOM * 2 + 2 * MOM * 2) * N * N * 2,
            transcendentals=0,
        ),
        name="mix_keep" if keep else "mix_send",
    )(left, right, node, weight, table, blocks)


def half_product(mixed, stack, out):
    parts = [
        jnp.dot(mixed[n], stack[...], preferred_element_type=F32).reshape(SNK, ROWS, 2 * N)
        for n in range(2)
    ]
    out[...] = jnp.concatenate(parts, 1).astype(out.dtype)


def send_kernel(tau_t, r0, r1, r2, r3, mixed, send, stack):
    tau = [
        tau_t[:, p].astype(F32).reshape(N, N).T.astype(BF16) for p in range(2)
    ]
    for d, block in enumerate((r0, r1, r2, r3)):
        real = jnp.dot(tau[0], block[0], preferred_element_type=F32) - jnp.dot(
            tau[1], block[1], preferred_element_type=F32
        )
        imag = jnp.dot(tau[0], block[1], preferred_element_type=F32) + jnp.dot(
            tau[1], block[0], preferred_element_type=F32
        )
        top, low = 2 * d * N, (2 * d + 1) * N
        stack[top : top + N, :N] = real.astype(BF16)
        stack[top : top + N, N:] = imag.astype(BF16)
        stack[low : low + N, :N] = (-imag).astype(BF16)
        stack[low : low + N, N:] = real.astype(BF16)
    half_product(mixed, stack, send)


def send_half(tau_t, right, mixed):
    vmem = pl.BlockSpec(memory_space=pltpu.VMEM)
    return pl.pallas_call(
        send_kernel,
        out_shape=(
            jax.ShapeDtypeStruct((SNK, 2 * ROWS, 2 * N), BF16),
            jax.ShapeDtypeStruct((DEEP, 2 * N), BF16),
        ),
        in_specs=[vmem] * 6,
        out_specs=(vmem, vmem),
        compiler_params=pltpu.CompilerParams(vmem_limit_bytes=VMEM_CAP),
        cost_estimate=pl.CostEstimate(
            flops=2 * (MOM * 4 + 2 * MOM * 4) * N * N * N,
            bytes_accessed=6 * 2**20,
            transcendentals=0,
        ),
        name="send_half",
    )(tau_t, *right, mixed)


def keep_half(mixed, stack):
    vmem = pl.BlockSpec(memory_space=pltpu.VMEM)
    return pl.pallas_call(
        half_product,
        out_shape=jax.ShapeDtypeStruct((SNK, 2 * ROWS, 2 * N), F32),
        in_specs=[vmem] * 2,
        out_specs=vmem,
        compiler_params=pltpu.CompilerParams(vmem_limit_bytes=VMEM_CAP),
        cost_estimate=pl.CostEstimate(
            flops=2 * 2 * MOM * 4 * N * N * N,
            bytes_accessed=5 * 2**20,
            transcendentals=0,
        ),
        name="keep_half",
    )(mixed, stack)


def device(y, c, x, z):
    return ((y * NC + c) * NX + x % NX) * NZ + z % NZ


def spread(block):
    y = lax.axis_index("y")
    lines = [(a, c, b) for a in range(NY) for c in range(NC) for b in range(NX)]
    own = lax.dynamic_index_in_dim(block, y, 0, keepdims=False)
    turns = [
        (device(b, (c + e) % NC, a, 4 * c), device(a, c, a + b, 4 * c + d))
        for a, c, b in lines
        for e, d in enumerate(POSTS)
    ]
    got = [lax.ppermute(own, ALL, turns)]
    for hops in LINES:
        pairs = [
            (device(a, c, b, 4 * c + post), device(a, c, b, 4 * c + d))
            for a, c, b in lines
            for post, d in zip(POSTS, hops)
        ]
        got.append(lax.ppermute(got[0], ALL, pairs))
    part = functools.reduce(jnp.add, got)
    pieces = {0: part}
    for d in ROUND:
        pieces[d] = lax.ppermute(part, "x", [(i, (i + d) % NX) for i in range(NX)])
    return [pieces[d] for d in range(NX)]


def shards(peram, meson_blocks, edge_left, edge_right, edge_node, edge_weight, weight_table):
    return contract(
        peram,
        meson_blocks,
        (edge_left, edge_right, edge_node, edge_weight, weight_table.T),
    )


def contract(peram, meson_blocks, edges):
    by_time = jnp.swapaxes(peram[0], 2, 3)
    tau_t = lax.all_to_all(by_time, ("x", "z"), split_axis=0, concat_axis=0, tiled=True)
    mixed_keep = mix(True, *edges, meson_blocks)
    mixed_send = mix(False, *edges, meson_blocks)
    right = spread(meson_blocks[0])
    send, stack = send_half(tau_t, right, mixed_send)
    got = lax.ppermute(send, "core", [(0, 1), (1, 0)])
    keep = keep_half(mixed_keep, stack)
    pair = (keep + got.astype(F32)).astype(BF16)
    times = lax.all_to_all(pair, ("x", "z"), split_axis=0, concat_axis=0, tiled=True)
    one = jnp.sum(times.astype(F32), 0)
    one = one.astype(BF16)
    copies = jnp.broadcast_to(one[None], (NY * NC,) + one.shape)
    every = lax.all_to_all(copies, ("y", "core"), split_axis=0, concat_axis=0, tiled=True)
    total = jnp.sum(every.astype(F32).reshape(NY, NC, 2, ROWS, 2, N), 0)
    return jnp.transpose(total, (2, 0, 1, 3, 4)).reshape(ROWS, NODES, 2, N).astype(BF16)


def solution(mesh):
    fine = Mesh(mesh.devices.reshape(NY, NC, NX, NZ), ALL)
    src, snk = ("y", "core"), ("x", "z")
    edges = P(src, snk, None)
    return jax.shard_map(
        shards,
        mesh=fine,
        in_specs=(
            P(src, None, None, None, snk),
            P(snk, None, None, None, None),
            edges,
            edges,
            edges,
            edges,
            P(),
        ),
        out_specs=P(snk, None, None, None),
        check_vma=False,
    )
```
